32 devices in a mesh: dp: 4 (over y, x), row: 4 (over z), col: 2 (over core).
Axes of the slice: x: 2, y: 2, z: 4, core: 2. Of those that a mesh axis runs over, the one named last changes fastest.
Arguments:
- tokens: bfloat16 [8, 1024, 1024], P(('dp', 'col'), 'row'), may hold values from -6 to 6
- lengths: int32 [8], P(('dp', 'col')), may hold values from 256 to 1024, as said below
- positions: int32 [8, 1024], P(('dp', 'col')), may hold values from 0 to 7164, as said below
- norm_attn: bfloat16 [1024], P('col'), may hold values from 0.25 to 1.75
- w_query: bfloat16 [1024, 1024], P('col', 'row'), may hold values from -0.1875 to 0.1875
- w_key: bfloat16 [1024, 512], P('col', 'row'), may hold values from -0.1875 to 0.1875
- w_value: bfloat16 [1024, 512], P('col', 'row'), may hold values from -0.1875 to 0.1875
- query_gain: bfloat16 [64], replicated, may hold values from 0.25 to 1.75
- key_gain: bfloat16 [64], replicated, may hold values from 0.25 to 1.75
- w_output: bfloat16 [1024, 1024], P('row', 'col'), may hold values from -0.75 to 0.75
- norm_ffn: bfloat16 [1024], P('col'), may hold values from 0.25 to 1.75
- w_gate: bfloat16 [1024, 4608], P('col', 'row'), may hold values from -0.1875 to 0.1875
- w_up: bfloat16 [1024, 4608], P('col', 'row'), may hold values from -0.1875 to 0.1875
- w_down: bfloat16 [4608, 1024], P('row', 'col'), may hold values from -0.09375 to 0.09375
- cotangent: bfloat16 [8, 1024, 1024], P(('dp', 'col'), 'row'), may hold values from -6 to 6
Outputs:
- block_out: bfloat16 [8, 1024, 1024], P(('dp', 'col'), 'row')
- input_grad: float32 [8, 1024, 1024], P(('dp', 'col'), 'row')
- d_norm_attn: float32 [1024], P('col')
- d_w_query: float32 [1024, 1024], P('col', 'row')
- d_w_key: float32 [1024, 512], P('col', 'row')
- d_w_value: float32 [1024, 512], P('col', 'row')
- d_query_gain: float32 [64], replicated
- d_key_gain: float32 [64], replicated
- d_w_output: float32 [1024, 1024], P('row', 'col')
- d_norm_ffn: float32 [1024], P('col')
- d_w_gate: float32 [1024, 4608], P('col', 'row')
- d_w_up: float32 [1024, 4608], P('col', 'row')
- d_w_down: float32 [4608, 1024], P('row', 'col')
The draws below stay inside these ranges and needn't reach their ends.
Inputs may be any that keep to these rules, and one draw needn't show every extreme that they name: Slots at or after lengths[s] of sequence s are padding; sequence 0 uses all 1024 slots and sequence 1 uses 1024 // 4. Within a sequence positions rise from slot to slot by 1, 2 or 3, starting below 4096.
All inputs are finite; a program needn't handle non-finite values.
Results may differ from the reference program's by a relative error of at most 0.018.
Values may be sent and summed in bfloat16 or wider, within the bound.
No kernel may reach another device: no remote copies, remote signals or barrier semaphores. Data moves between devices by JAX's collectives and lax.ppermute only.
A program may use at most 128 MiB of HBM per device.

```python
import math
import jax
import jax.numpy as jnp
from jax import lax

D = 1024
FF = 4608
HQ = 16
KV = 8
HD = 64
SLOT = 1024
QB = 512
SEQS = 8


def draw_lengths(key, part):
    values = jax.random.randint(key, (SEQS,), SLOT // 4, SLOT + 1)
    values = values.at[0].set(SLOT)
    values = values.at[1].set(SLOT // 4)
    return values.astype(jnp.int32)


def draw_positions(key, part):
    start_key = jax.random.fold_in(key, 11)
    step_key = jax.random.fold_in(key, 23)
    starts = jax.random.randint(start_key, (SEQS,), 0, 4096)
    starts = starts.at[0].set(4095)
    starts = starts.at[1].set(0)
    increments = jax.random.randint(step_key, (SEQS, SLOT), 1, 4)
    increments = increments.at[0].set(3)
    increments = increments.at[:, 0].set(0)
    offsets = jnp.cumsum(increments, axis=1)
    return (starts[:, None] + offsets).astype(jnp.int32)


def spiked(result, rng, source, target, parts, factor):
    owner, partner = [(jnp.arange(result.shape[dim]) // (result.shape[dim] // parts)).reshape([-1 if axis == dim else 1 for axis in range(result.ndim)]) for dim in (source, target)]
    chosen = jax.random.permutation(rng, parts)[partner]
    strong = (owner == chosen) | (owner == (partner + parts // 2) % parts)
    return jnp.where(strong, factor * result, result)


def block_scale(key, extent, cuts, low, largest):
    gain = 1.0
    for axis_at, parts in cuts:
        steps = jax.random.uniform(jax.random.fold_in(jax.random.fold_in(key, 6), axis_at), (parts,), jnp.float32, low / len(cuts), largest / len(cuts))
        gain = gain * jnp.repeat(jnp.exp(steps), extent[axis_at] // parts).reshape((-1,) + (1,) * (len(extent) - 1 - axis_at))
    return gain


def scatter_about(stream_key, shape, width, limit, pieces=(), kind=jnp.bfloat16):
    loudness = block_scale(stream_key, shape, pieces, -0.22, 0.18) if pieces else 1.0
    result = jax.random.normal(stream_key, shape, jnp.float32) * width * loudness
    return jnp.minimum(jnp.maximum(result, -limit), limit).astype(kind)


def bell_draw_with(own_key, shape, width, bound, shards, heavy, kind=jnp.bfloat16):
    entries = width * jax.random.normal(own_key, shape, jnp.float32)
    if shards:
        entries = entries * block_scale(own_key, shape, shards, -0.22, 0.18)
    return jnp.clip(spiked(entries, jax.random.fold_in(own_key, 3), *heavy), -bound, bound).astype(kind)


def setup_inputs(seed: int = 0) -> dict:
    seeds = jax.random.split(jax.random.key(seed), 16)
    tokens = scatter_about(seeds[0], (SEQS, SLOT, D), 1.0, 6.0, ((0, 8), (1, 4)))
    lengths = draw_lengths(jax.random.fold_in(seeds[15], 71), 0)
    positions = draw_positions(jax.random.fold_in(seeds[15], 71), 0)
    norm_attn = jnp.clip(1.0 + 0.15 * jax.random.normal(seeds[3], (D,), jnp.float32), 0.25, 1.75).astype(jnp.bfloat16)
    w_query = scatter_about(seeds[4], (D, HQ * HD), D ** -0.5, 0.1875, ((0, 2), (1, 4)))
    w_key = scatter_about(seeds[5], (D, KV * HD), D ** -0.5, 0.1875, ((0, 2), (1, 4)))
    w_value = scatter_about(seeds[6], (D, KV * HD), D ** -0.5, 0.1875, ((0, 2), (1, 4)))
    query_gain = jnp.clip(1.0 + 0.15 * jax.random.normal(seeds[7], (HD,), jnp.float32), 0.25, 1.75).astype(jnp.bfloat16)
    key_gain = jnp.clip(1.0 + 0.15 * jax.random.normal(seeds[8], (HD,), jnp.float32), 0.25, 1.75).astype(jnp.bfloat16)
    w_output = scatter_about(seeds[9], (HQ * HD, D), (HQ * HD // 16) ** -0.5, 0.75, ((0, 4), (1, 2)))
    norm_ffn = jnp.clip(1.0 + 0.15 * jax.random.normal(seeds[10], (D,), jnp.float32), 0.25, 1.75).astype(jnp.bfloat16)
    w_gate = scatter_about(seeds[11], (D, FF), D ** -0.5, 0.1875, ((0, 2), (1, 4)))
    w_up = scatter_about(seeds[12], (D, FF), D ** -0.5, 0.1875, ((0, 2), (1, 4)))
    w_down = scatter_about(seeds[13], (FF, D), FF ** -0.5, 0.09375, ((0, 4), (1, 2)))
    cotangent = bell_draw_with(seeds[14], (SEQS, SLOT, D), 1.0, 6.0, ((0, 8), (1, 4)), (0, 2, 8, 2.0))
    return {"tokens": tokens, "lengths": lengths, "positions": positions, "norm_attn": norm_attn, "w_query": w_query, "w_key": w_key, "w_value": w_value, "query_gain": query_gain, "key_gain": key_gain, "w_output": w_output, "norm_ffn": norm_ffn, "w_gate": w_gate, "w_up": w_up, "w_down": w_down, "cotangent": cotangent}


EPSILON = 1e-05
ROPE_BASE = 1000000.0
HIGHEST = lax.Precision.HIGHEST

@jax.custom_vjp
def low(v):
    return lax.optimization_barrier(v.astype(jnp.bfloat16)).astype(jnp.float32)

@jax.custom_vjp
def low_back(v):
    return v

def low_keep(v):
    return (low(v), None)

def low_pass(kept, grad):
    return (grad,)

def back_keep(v):
    return (v, None)

def back_low(kept, grad):
    return (low(grad),)
low.defvjp(low_keep, low_pass)
low_back.defvjp(back_keep, back_low)

def rms_scale(values):
    return values * lax.rsqrt(lax.optimization_barrier(jnp.mean(values * values, axis=-1, keepdims=True)) + EPSILON)

def rope_tables(places):
    half_dim = HD // 2
    inv_freq = ROPE_BASE ** (-(jnp.arange(half_dim, dtype=jnp.float32) * 2.0 / HD))
    angles = places.astype(jnp.float32)[:, None] * inv_freq[None, :]
    return (jnp.cos(angles), jnp.sin(angles))

def rotate(values, cosine, sine_tab):
    half_dim = values.shape[-1] // 2
    front_half = values[..., :half_dim]
    back_half = values[..., half_dim:]
    cos_col = cosine[:, None, :]
    sin_col = sine_tab[:, None, :]
    return jnp.concatenate([front_half * cos_col - back_half * sin_col, back_half * cos_col + front_half * sin_col], axis=-1)

def heads_prep(query_in, key_in, query_gain, key_gain, cosine, sine_tab):
    num_rows = query_in.shape[0]
    q_heads = rms_scale(query_in.reshape(num_rows, -1, HD)) * query_gain
    k_heads = rms_scale(key_in.reshape(num_rows, -1, HD)) * key_gain
    return (rotate(q_heads, cosine, sine_tab), rotate(k_heads, cosine, sine_tab))

def attend(q_rot, k_rot, v_heads, length):
    seq_len = q_rot.shape[0]
    groups = HQ // KV
    q_group = q_rot.reshape(seq_len, KV, groups, HD)
    key_pos = jnp.arange(seq_len, dtype=jnp.int32)
    scale_val = 1.0 / math.sqrt(HD)

    def one_block(block_num):
        start_row = (block_num * QB).astype(jnp.int32)
        q_block = lax.dynamic_slice_in_dim(q_group, start_row, QB, 0)
        scores = jnp.einsum('qkgd,tkd->kgqt', q_block, k_rot, precision=HIGHEST) * scale_val
        rows_pos = start_row + jnp.arange(QB, dtype=jnp.int32)
        allowed = (key_pos[None, :] <= rows_pos[:, None]) & (key_pos[None, :] < length)
        scores = low_back(jnp.where(allowed, scores, -1e+30))
        prob_vals = low(jax.nn.softmax(scores, axis=-1))
        return jnp.einsum('kgqt,tkd->qkgd', prob_vals, v_heads, precision=HIGHEST)
    blocks = lax.map(jax.checkpoint(one_block), jnp.arange(seq_len // QB, dtype=jnp.int32))
    return blocks.reshape(seq_len, HQ * HD)

def layer(inputs, norm_attn, w_query, w_key, w_value, query_gain, key_gain, w_output, norm_ffn, w_gate, w_up, w_down, places, length):
    seq_len = inputs.shape[0]
    normed = low(rms_scale(inputs) * norm_attn)
    query_in = low_back(jnp.dot(normed, w_query, precision=HIGHEST))
    key_in = low_back(jnp.dot(normed, w_key, precision=HIGHEST))
    value_in = low_back(jnp.dot(normed, w_value, precision=HIGHEST))
    cosine, sine_tab = rope_tables(places)
    q_rot, k_rot = heads_prep(query_in, key_in, query_gain, key_gain, cosine, sine_tab)
    attended = attend(low(q_rot), low(k_rot), low(value_in).reshape(seq_len, KV, HD), length)
    merged = low_back(low(attended))
    branch = low_back(jnp.dot(merged, w_output, precision=HIGHEST))
    hidden_in = inputs + branch
    normed_two = low(rms_scale(hidden_in) * norm_ffn)
    gate_in = low_back(jnp.dot(normed_two, w_gate, precision=HIGHEST))
    up_in = low_back(jnp.dot(normed_two, w_up, precision=HIGHEST))
    inner = low(jax.nn.silu(gate_in) * up_in)
    ffn_out = low_back(jnp.dot(inner, w_down, precision=HIGHEST))
    return hidden_in + ffn_out

def reference(tokens, lengths, positions, norm_attn, w_query, w_key, w_value, query_gain, key_gain, w_output, norm_ffn, w_gate, w_up, w_down, cotangent):
    params = tuple((weight_arr.astype(jnp.float32) for weight_arr in (norm_attn, w_query, w_key, w_value, query_gain, key_gain, w_output, norm_ffn, w_gate, w_up, w_down)))

    def per_seq(totals, items):
        seq_tokens, seq_length, seq_places, seq_cot = items

        def apply_layer(seq_in, g_one, w_qq, w_kk, w_vv, g_qq, g_kk, w_oo, g_two, w_gg, w_uu, w_dd):
            return layer(seq_in, g_one, w_qq, w_kk, w_vv, g_qq, g_kk, w_oo, g_two, w_gg, w_uu, w_dd, seq_places, seq_length)
        out_val, pullback = jax.vjp(apply_layer, seq_tokens.astype(jnp.float32), params[0], params[1], params[2], params[3], params[4], params[5], params[6], params[7], params[8], params[9], params[10])
        grads = pullback(seq_cot.astype(jnp.float32))
        new_totals = tuple((total_val + grad_val for total_val, grad_val in zip(totals, grads[1:])))
        return (new_totals, (out_val.astype(jnp.bfloat16), grads[0]))
    zero_totals = tuple((jnp.zeros(weight_arr.shape, jnp.float32) for weight_arr in params))
    totals, outputs = lax.scan(per_seq, zero_totals, (tokens, lengths, positions, cotangent))
    return (outputs[0], outputs[1], totals[0], totals[1], totals[2], totals[3], totals[4], totals[5], totals[6], totals[7], totals[8], totals[9], totals[10])
```

```python
import functools

import jax
import jax.numpy as jnp
from jax import lax
from jax.experimental import pallas as pl
from jax.experimental.pallas import tpu as pltpu
from jax.sharding import PartitionSpec as P

HD = 64
EPSILON = 1e-05
ROPE_BASE = 1000000.0
MASKED = -1e30
F32 = jnp.float32
BF16 = jnp.bfloat16


def dot(a, b):
    return jnp.dot(a, b, preferred_element_type=F32)


def dot_nt(a, b):
    return lax.dot_general(a, b, (((1,), (1,)), ((), ())), preferred_element_type=F32)


def dot_tn(a, b):
    return lax.dot_general(a, b, (((0,), (0,)), ((), ())), preferred_element_type=F32)


def swap_perm(size, bit):
    return [(i, i ^ bit) for i in range(size)]


def butterfly_sum(values, axes):
    for axis in axes:
        size = lax.axis_size(axis)
        bit = 1
        while bit < size:
            values = values + lax.ppermute(values, axis, swap_perm(size, bit))
            bit *= 2
    return values


def col_gather(block, axis):
    if lax.axis_size("col") != 2:
        return lax.all_gather(block, "col", axis=axis, tiled=True)
    other = lax.ppermute(block, "col", swap_perm(2, 1))
    first = lax.axis_index("col") == 0
    return jnp.concatenate(
        [jnp.where(first, block, other), jnp.where(first, other, block)], axis=axis
    )


def col_scatter_sum(grad):
    if lax.axis_size("col") != 2:
        return lax.psum_scatter(grad, "col", scatter_dimension=0, tiled=True)
    half = grad.shape[0] // 2
    first = lax.axis_index("col") == 0
    keep = jnp.where(first, grad[:half], grad[half:])
    send = jnp.where(first, grad[half:], grad[:half])
    return (
        keep.astype(F32) + lax.ppermute(send, "col", swap_perm(2, 1)).astype(F32)
    ).astype(BF16)


def dp_reduce(grad):
    size = lax.axis_size("dp")
    if size != 4:
        return lax.psum(grad, "dp")
    place = lax.axis_index("dp")
    rows = grad.shape[0] // 2
    parts = []
    for piece, bits in ((grad[:rows], (1, 2)), (grad[rows:], (2, 1))):
        for bit in bits:
            half = piece.shape[0] // 2
            low = (place & bit) == 0
            keep = jnp.where(low, piece[:half], piece[half:])
            send = jnp.where(low, piece[half:], piece[:half])
            other = lax.ppermute(send, "dp", swap_perm(4, bit))
            piece = (keep.astype(F32) + other.astype(F32)).astype(BF16)
        for bit in bits[::-1]:
            low = (place & bit) == 0
            other = lax.ppermute(piece, "dp", swap_perm(4, bit))
            piece = jnp.concatenate(
                [jnp.where(low, piece, other), jnp.where(low, other, piece)], axis=0
            )
        parts.append(piece)
    return jnp.concatenate(parts, axis=0)


EVEN = [(0, 1), (1, 0), (2, 3), (3, 2)]
ODD = [(1, 2), (2, 1)]


def even(values):
    return lax.ppermute(values, "row", EVEN)


def odd(values):
    return lax.ppermute(values, "row", ODD)


def row_slots():
    place = lax.axis_index("row")
    left = place < 2
    return place, place ^ 1, jnp.where(left, 2, 1), jnp.where(left, 3, 0)


def row_gather(block):
    if lax.axis_size("row") != 4:
        return lax.all_gather(block, "row", axis=0, tiled=True)
    rows = block.shape[0]
    place = lax.axis_index("row")
    inner = (place == 1) | (place == 2)
    near = even(block)
    other = odd(block)
    third = even(other)
    fourth = odd(near)
    last = even(fourth)
    slots = (block, near, jnp.where(inner, other, third), jnp.where(inner, fourth, last))
    total = jnp.zeros((4 * rows,) + block.shape[1:], block.dtype)
    for slot, index in zip(slots, row_slots()):
        total = lax.dynamic_update_slice_in_dim(total, slot, index * rows, 0)
    return total


def row_scatter_sum(total):
    if lax.axis_size("row") != 4:
        return lax.psum_scatter(total, "row", scatter_dimension=0, tiled=True).astype(F32)
    rows = total.shape[0] // 4
    own, near, third, fourth = (
        lax.dynamic_slice_in_dim(total, index * rows, rows, 0) for index in row_slots()
    )

    def add(a, b):
        return (a.astype(F32) + b.astype(F32)).astype(BF16)

    far = odd(add(fourth, even(fourth)))
    side = odd(add(third, even(third)))
    side_even = even(add(near, far))
    return own.astype(F32) + side.astype(F32) + side_even.astype(F32)


def output_gather(block):
    rows, width = block.shape
    dp = lax.axis_size("dp")
    part = rows // dp
    mine = lax.dynamic_slice_in_dim(block, lax.axis_index("dp") * part, part, 0)
    if dp != 4 or lax.axis_size("row") != 4:
        half = lax.all_gather(block, "row", axis=0, tiled=True)
    else:
        piece = row_gather(mine).reshape(4, 1, part, width)
        place = lax.axis_index("dp")
        for bit in (1, 2):
            low = (place & bit) == 0
            other = lax.ppermute(piece, "dp", swap_perm(4, bit))
            piece = jnp.concatenate(
                [jnp.where(low, piece, other), jnp.where(low, other, piece)], axis=1
            )
        half = piece.reshape(4 * rows, width)
    return col_gather(half, 1)


def full_spec(shape):
    zeros = (0,) * len(shape)
    return pl.BlockSpec(shape, lambda i: zeros)


def attend_fwd_kernel(
    len_ref, x_ref, gain_ref, w_ref, qg_ref, kg_ref, cos_ref, sin_ref,
    a1_ref, pre_ref, qt_ref, kt_ref, k_ref, v_ref, o_ref, lse_ref,
    k_s, vt_s, qt_s, ot_s,
):
    i = pl.program_id(0)
    rows = x_ref.shape[0]
    nkv = kt_ref.shape[0]
    nq = qt_ref.shape[0]
    x = x_ref[...].astype(F32)
    r1 = lax.rsqrt(jnp.mean(x * x, axis=-1, keepdims=True) + EPSILON)
    a1 = (x * r1 * gain_ref[...]).astype(BF16)
    a1_ref[...] = a1
    qkv_t = dot(a1, w_ref[...]).T
    heads = qkv_t[: (nq + nkv) * HD].reshape(nq + nkv, HD, rows)
    pre_ref[...] = heads
    normed = heads * lax.rsqrt(jnp.mean(heads * heads, axis=1, keepdims=True) + EPSILON)
    gains = jnp.concatenate(
        [jnp.broadcast_to(qg_ref[...][None], (nq, HD, 1)), jnp.broadcast_to(kg_ref[...][None], (nkv, HD, 1))],
        axis=0,
    )
    normed = normed * gains
    cos = cos_ref[...][None]
    sin = sin_ref[...][None]
    front = normed[:, : HD // 2]
    back = normed[:, HD // 2 :]
    rot = jnp.concatenate([front * cos - back * sin, back * cos + front * sin], axis=1)
    qt = (rot[:nq].astype(BF16).astype(F32) * HD**-0.5).astype(BF16)
    qt_s[...] = qt
    qt_ref[...] = qt
    kt = rot[nq:]
    kt_ref[...] = kt.astype(BF16)
    k_rows = kt.reshape(nkv * HD, rows).T.astype(BF16)
    v_t = qkv_t[(nq + nkv) * HD :]
    v_rows = v_t.T.astype(BF16)
    here = pl.ds(pl.multiple_of(i * rows, rows), rows)
    for g in range(nkv):
        part = k_rows[:, g * HD : (g + 1) * HD]
        k_ref[g] = part
        k_s[g, here, :] = part
        v_ref[g] = v_rows[:, g * HD : (g + 1) * HD]
        vt_s[g, :, here] = v_t[g * HD : (g + 1) * HD].astype(BF16)
    bound = jnp.minimum(
        i * rows + lax.broadcasted_iota(jnp.int32, (1, rows), 1) + 1, len_ref[0]
    )
    for case in range(pl.num_programs(0)):

        @pl.when(i == case)
        def _(case=case):
            seen = (case + 1) * rows
            allowed = lax.broadcasted_iota(jnp.int32, (seen, rows), 0) < bound

            def one_head(h, carry):
                g = h // (nq // nkv)
                scores = dot(k_s[g, :seen, :], qt_s[h])
                scores = jnp.where(allowed, scores, MASKED)
                top = jnp.max(scores, axis=0, keepdims=True)
                shifted = jnp.exp(scores - top)
                total = jnp.sum(shifted, axis=0, keepdims=True)
                ot = dot(vt_s[g, :, :seen], shifted.astype(BF16))
                ot_s[h] = ot / total
                lse_ref[h] = top + jnp.log(total)
                return carry

            lax.fori_loop(0, nq, one_head, 0)

    o_ref[...] = ot_s[...].reshape(nq * HD, rows).T.astype(BF16)


def attend_fwd(x_all, length, gain, w_qkv, q_gain, k_gain, cos_t, sin_t, nq, nkv, blocks):
    seq, width = x_all.shape
    rows = seq // blocks
    heads = nq + nkv
    outs = (
        jax.ShapeDtypeStruct((seq, width), BF16),
        jax.ShapeDtypeStruct((heads, HD, seq), F32),
        jax.ShapeDtypeStruct((nq, HD, seq), BF16),
        jax.ShapeDtypeStruct((nkv, HD, seq), BF16),
        jax.ShapeDtypeStruct((nkv, seq, HD), BF16),
        jax.ShapeDtypeStruct((nkv, seq, HD), BF16),
        jax.ShapeDtypeStruct((seq, nq * HD), BF16),
        jax.ShapeDtypeStruct((nq, 1, seq), F32),
    )
    return pl.pallas_call(
        attend_fwd_kernel,
        grid=(blocks,),
        in_specs=[
            pl.BlockSpec(memory_space=pltpu.SMEM),
            pl.BlockSpec((rows, width), lambda i: (i, 0)),
            full_spec((1, width)),
            full_spec(w_qkv.shape),
            full_spec((HD, 1)),
            full_spec((HD, 1)),
            pl.BlockSpec((HD // 2, rows), lambda i: (0, i)),
            pl.BlockSpec((HD // 2, rows), lambda i: (0, i)),
        ],
        out_specs=(
            pl.BlockSpec((rows, width), lambda i: (i, 0)),
            pl.BlockSpec((heads, HD, rows), lambda i: (0, 0, i)),
            pl.BlockSpec((nq, HD, rows), lambda i: (0, 0, i)),
            pl.BlockSpec((nkv, HD, rows), lambda i: (0, 0, i)),
            pl.BlockSpec((nkv, rows, HD), lambda i: (0, i, 0)),
            pl.BlockSpec((nkv, rows, HD), lambda i: (0, i, 0)),
            pl.BlockSpec((rows, nq * HD), lambda i: (i, 0)),
            pl.BlockSpec((nq, 1, rows), lambda i: (0, 0, i)),
        ),
        out_shape=outs,
        scratch_shapes=[
            pltpu.VMEM((nkv, seq, HD), BF16),
            pltpu.VMEM((nkv, HD, seq), BF16),
            pltpu.VMEM((nq, HD, rows), BF16),
            pltpu.VMEM((nq, HD, rows), F32),
        ],
        compiler_params=pltpu.CompilerParams(vmem_limit_bytes=40 << 20),
        cost_estimate=pl.CostEstimate(
            flops=2 * seq * width * w_qkv.shape[1] + 4 * seq * seq * nq * HD,
            bytes_accessed=10 << 20,
            transcendentals=nq * seq * seq,
        ),
        name="attend_fwd",
    )(length, x_all, gain, w_qkv, q_gain, k_gain, cos_t, sin_t)


def ffn_kernel(
    x_ref, o_ref, c_ref, gain_ref, wo_ref, wg_ref, wu_ref, wd_ref,
    h_ref, a2_ref, hid_ref, dgu_ref, da2_ref, dn_ref,
):
    parts, rows, span = o_ref.shape
    width = x_ref.shape[1]
    ff = wg_ref.shape[1]
    att = dot(o_ref[0], wo_ref[:span])
    for z in range(1, parts):
        att = att + dot(o_ref[z], wo_ref[z * span : (z + 1) * span])
    h = x_ref[...].astype(F32) + att
    h_ref[...] = h
    r2 = lax.rsqrt(jnp.mean(h * h, axis=-1, keepdims=True) + EPSILON)
    u2 = h * r2
    a2 = (u2 * gain_ref[...]).astype(BF16)
    a2_ref[...] = a2
    gate = dot(a2, wg_ref[...])
    up = dot(a2, wu_ref[...])
    dhid = dot_nt(c_ref[...], wd_ref[...])
    sig = 1.0 / (1.0 + jnp.exp(-gate))
    silu = gate * sig
    hid_ref[...] = (silu * up).astype(BF16)
    dgate = (dhid * up * sig * (1.0 + gate * (1.0 - sig))).astype(BF16)
    dup = (dhid * silu).astype(BF16)
    dgu_ref[:, :ff] = dgate
    dgu_ref[:, ff:] = dup
    da2 = dot_nt(dgate, wg_ref[...]) + dot_nt(dup, wu_ref[...])
    da2_ref[...] = da2.astype(BF16)
    part = jnp.sum((da2 * u2).reshape(rows // 8, 8, width), axis=0)

    @pl.when(pl.program_id(0) == 0)
    def _():
        dn_ref[...] = jnp.zeros_like(dn_ref)

    dn_ref[...] += part


def ffn(x_all, o_parts, c_all, gain, w_out, w_gate, w_up, w_down, blocks):
    seq, width = x_all.shape
    rows = seq // blocks
    parts, _, span = o_parts.shape
    ff = w_gate.shape[1]
    by_row = lambda i: (i, 0)
    return pl.pallas_call(
        ffn_kernel,
        grid=(blocks,),
        in_specs=[
            pl.BlockSpec((rows, width), by_row),
            pl.BlockSpec((parts, rows, span), lambda i: (0, i, 0)),
            pl.BlockSpec((rows, width), by_row),
            full_spec((1, width)),
            full_spec(w_out.shape),
            full_spec(w_gate.shape),
            full_spec(w_up.shape),
            full_spec(w_down.shape),
        ],
        out_specs=(
            pl.BlockSpec((rows, width), by_row),
            pl.BlockSpec((rows, width), by_row),
            pl.BlockSpec((rows, ff), by_row),
            pl.BlockSpec((rows, 2 * ff), by_row),
            pl.BlockSpec((rows, width), by_row),
            full_spec((8, width)),
        ),
        out_shape=(
            jax.ShapeDtypeStruct((seq, width), F32),
            jax.ShapeDtypeStruct((seq, width), BF16),
            jax.ShapeDtypeStruct((seq, ff), BF16),
            jax.ShapeDtypeStruct((seq, 2 * ff), BF16),
            jax.ShapeDtypeStruct((seq, width), BF16),
            jax.ShapeDtypeStruct((8, width), F32),
        ),
        compiler_params=pltpu.CompilerParams(vmem_limit_bytes=56 << 20),
        cost_estimate=pl.CostEstimate(
            flops=2 * seq * width * (width + 5 * ff), bytes_accessed=30 << 20, transcendentals=seq * ff
        ),
        name="ffn",
    )(x_all, o_parts, c_all, gain, w_out, w_gate, w_up, w_down)


def attend_back_kernel(
    len_ref, dhb_ref, x_ref, wo_ref, w_ref, qt_ref, lse_ref, k_ref, v_ref, kt_ref, pre_ref,
    qg_ref, kg_ref, cos_ref, sin_ref,
    dqkv_ref, da1_ref, dn_ref, dg_ref,
    dk_s, dv_s, q_s, do_s, dot_s, dqt_s,
):
    step = pl.program_id(0)
    blocks = pl.num_programs(0)
    i = blocks - 1 - step
    rows, width = x_ref.shape
    nq = qt_ref.shape[0]
    nkv = kt_ref.shape[0]
    groups = nq // nkv

    @pl.when(step == 0)
    def _():
        dk_s[...] = jnp.zeros_like(dk_s)
        dv_s[...] = jnp.zeros_like(dv_s)
        dn_ref[...] = jnp.zeros_like(dn_ref)
        dg_ref[...] = jnp.zeros_like(dg_ref)

    d_out = dot_nt(dhb_ref[...], wo_ref[...]).astype(BF16).astype(F32)
    dot_s[...] = d_out.T.reshape(nq, HD, rows).astype(BF16)
    d_out = d_out.astype(BF16)
    q_rows = qt_ref[...].astype(F32).reshape(nq * HD, rows).T.astype(BF16)
    for h in range(nq):
        do_s[h] = d_out[:, h * HD : (h + 1) * HD]
        q_s[h] = q_rows[:, h * HD : (h + 1) * HD]
    bound = jnp.minimum(
        i * rows + lax.broadcasted_iota(jnp.int32, (1, rows), 1) + 1, len_ref[0]
    )
    for case in range(blocks):

        @pl.when(i == case)
        def _(case=case):
            seen = (case + 1) * rows
            allowed = lax.broadcasted_iota(jnp.int32, (seen, rows), 0) < bound

            def one_head(h, carry):
                g = h // groups
                scores = dot(k_ref[g, :seen, :], qt_ref[h])
                prob = jnp.where(allowed, jnp.exp(scores - lse_ref[h]), 0.0)
                dprob = dot(v_ref[g, :seen, :], dot_s[h])
                inner = jnp.sum(prob * dprob, axis=0, keepdims=True)
                ds = (prob * (dprob - inner)).astype(BF16)
                dqt_s[h] = dot(kt_ref[g, :, :seen], ds) * HD**-0.5
                dk_s[g, :seen, :] += dot(ds, q_s[h])
                dv_s[g, :seen, :] += dot(prob.astype(BF16), do_s[h])
                return carry

            lax.fori_loop(0, nq, one_head, 0)

    here = pl.ds(pl.multiple_of(i * rows, rows), rows)
    dk_t = jnp.concatenate([dk_s[g, here, :] for g in range(nkv)], axis=1).T
    dv = jnp.concatenate([dv_s[g, here, :] for g in range(nkv)], axis=1).astype(BF16)
    rot = jnp.concatenate([dqt_s[...], dk_t.reshape(nkv, HD, rows)], axis=0)
    cos = cos_ref[...][None]
    sin = sin_ref[...][None]
    front = rot[:, : HD // 2]
    back = rot[:, HD // 2 :]
    dn = jnp.concatenate([front * cos + back * sin, back * cos - front * sin], axis=1)
    pre = pre_ref[...]
    scale = lax.rsqrt(jnp.mean(pre * pre, axis=1, keepdims=True) + EPSILON)
    unit = pre * scale
    grads = dn * unit
    dg_ref[0] += jnp.sum(grads[:nq], axis=0)
    dg_ref[1] += jnp.sum(grads[nq:], axis=0)
    gains = jnp.concatenate(
        [jnp.broadcast_to(qg_ref[...][None], (nq, HD, 1)), jnp.broadcast_to(kg_ref[...][None], (nkv, HD, 1))],
        axis=0,
    )
    e = dn * gains
    dpre = scale * (e - unit * jnp.mean(e * unit, axis=1, keepdims=True))
    dqk = dpre.reshape((nq + nkv) * HD, rows).T.astype(BF16)
    dqkv = jnp.concatenate([dqk, dv], axis=1)
    dqkv_ref[...] = dqkv
    da1 = dot_nt(dqkv, w_ref[...])
    da1_ref[...] = da1.astype(BF16)
    x = x_ref[...].astype(F32)
    u1 = x * lax.rsqrt(jnp.mean(x * x, axis=-1, keepdims=True) + EPSILON)
    dn_ref[...] += jnp.sum((da1 * u1).reshape(rows // 8, 8, width), axis=0)


def attend_back(
    dhb, length, x_all, w_out, w_qkv, q_t, lse, k_rows, v_rows, k_t, pre, q_gain, k_gain, cos_t, sin_t, blocks
):
    seq, width = x_all.shape
    rows = seq // blocks
    nq = q_t.shape[0]
    nkv = k_t.shape[0]
    heads = nq + nkv
    last = blocks - 1
    by_row = lambda i: (last - i, 0)
    by_lane = lambda i: (0, 0, last - i)
    return pl.pallas_call(
        attend_back_kernel,
        grid=(blocks,),
        in_specs=[
            pl.BlockSpec(memory_space=pltpu.SMEM),
            pl.BlockSpec((rows, width), by_row),
            pl.BlockSpec((rows, width), by_row),
            full_spec(w_out.shape),
            full_spec(w_qkv.shape),
            pl.BlockSpec((nq, HD, rows), by_lane),
            pl.BlockSpec((nq, 1, rows), by_lane),
            full_spec(k_rows.shape),
            full_spec(v_rows.shape),
            full_spec(k_t.shape),
            pl.BlockSpec((heads, HD, rows), by_lane),
            full_spec((HD, 1)),
            full_spec((HD, 1)),
            pl.BlockSpec((HD // 2, rows), lambda i: (0, last - i)),
            pl.BlockSpec((HD // 2, rows), lambda i: (0, last - i)),
        ],
        out_specs=(
            pl.BlockSpec((rows, w_qkv.shape[1]), by_row),
            pl.BlockSpec((rows, width), by_row),
            full_spec((8, width)),
            full_spec((2, HD, rows)),
        ),
        out_shape=(
            jax.ShapeDtypeStruct((seq, w_qkv.shape[1]), BF16),
            jax.ShapeDtypeStruct((seq, width), BF16),
            jax.ShapeDtypeStruct((8, width), F32),
            jax.ShapeDtypeStruct((2, HD, rows), F32),
        ),
        scratch_shapes=[
            pltpu.VMEM((nkv, seq, HD), F32),
            pltpu.VMEM((nkv, seq, HD), F32),
            pltpu.VMEM((nq, rows, HD), BF16),
            pltpu.VMEM((nq, rows, HD), BF16),
            pltpu.VMEM((nq, HD, rows), BF16),
            pltpu.VMEM((nq, HD, rows), F32),
        ],
        compiler_params=pltpu.CompilerParams(vmem_limit_bytes=48 << 20),
        cost_estimate=pl.CostEstimate(
            flops=4 * seq * width * w_qkv.shape[1] + 10 * seq * seq * nq * HD,
            bytes_accessed=12 << 20,
            transcendentals=nq * seq * seq,
        ),
        name="attend_back",
    )(length, dhb, x_all, w_out, w_qkv, q_t, lse, k_rows, v_rows, k_t, pre, q_gain, k_gain, cos_t, sin_t)


def local(
    tokens, lengths, positions, norm_attn, w_query, w_key, w_value, query_gain, key_gain,
    w_output, norm_ffn, w_gate, w_up, w_down, cotangent,
):
    x_own = tokens[0]
    c_own = cotangent[0]
    own_rows, width = x_own.shape
    seq = positions.shape[1]
    blocks = seq // own_rows
    nq = w_query.shape[1] // HD
    nkv = w_key.shape[1] // HD
    row_start = lax.axis_index("row") * own_rows

    x_all = lax.all_gather(x_own, "row", axis=0, tiled=True)

    gains = jnp.stack([norm_attn, norm_ffn])
    w_qkv = col_gather(jnp.concatenate([w_query, w_key, w_value], axis=1), 0)
    gains = col_gather(gains, 1).astype(F32)
    w_gate = col_gather(w_gate, 0)
    w_up = col_gather(w_up, 0)
    w_down = col_gather(w_down, 1)
    w_out_all = output_gather(w_output)
    w_out = col_gather(w_output, 1)
    gain_attn = gains[0:1]
    gain_ffn = gains[1:2]
    q_gain = query_gain.astype(F32)[:, None]
    k_gain = key_gain.astype(F32)[:, None]
    inv_freq = ROPE_BASE ** (-(jnp.arange(HD // 2, dtype=F32) * 2.0 / HD))
    angles = inv_freq[:, None] * positions[0].astype(F32)[None, :]
    cos_t = jnp.cos(angles)
    sin_t = jnp.sin(angles)

    a1, pre, q_t, k_t, k_rows, v_rows, merged, lse = attend_fwd(
        x_all, lengths, gain_attn, w_qkv, q_gain, k_gain, cos_t, sin_t, nq, nkv, blocks
    )
    o_parts = lax.all_gather(merged, "row", axis=0, tiled=False)
    c_all = row_gather(c_own)
    h_all, a2, hid, dgu, da2_part, dnorm_ffn = ffn(
        x_all, o_parts, c_all, gain_ffn, w_out_all, w_gate, w_up, w_down, blocks
    )
    da2 = lax.psum_scatter(da2_part, "row", scatter_dimension=0, tiled=True).astype(F32)

    ff = w_up.shape[1]
    ffn_part = dot(hid, w_down).astype(BF16)
    d_gu = col_scatter_sum(dot_tn(a2, dgu).astype(BF16))
    d_down = col_scatter_sum(dot_tn(c_all, hid).astype(BF16))
    d_ffn = dp_reduce(jnp.concatenate([d_gu, d_down], axis=1)).astype(F32)

    h_own = lax.dynamic_slice_in_dim(h_all, row_start, own_rows, 0)
    r2 = lax.rsqrt(jnp.mean(h_own * h_own, axis=-1, keepdims=True) + EPSILON)
    u2 = h_own * r2
    e2 = da2 * gain_ffn
    dh = c_own.astype(F32) + r2 * (e2 - u2 * jnp.mean(e2 * u2, axis=-1, keepdims=True))
    dhb_all = lax.all_gather(dh.astype(BF16), "row", axis=0, tiled=True)

    block_out = (h_own + row_scatter_sum(ffn_part)).astype(BF16)

    dqkv, da1_part, dnorm_attn, dgains = attend_back(
        dhb_all, lengths, x_all, w_out, w_qkv, q_t, lse, k_rows, v_rows, k_t, pre,
        q_gain, k_gain, cos_t, sin_t, blocks,
    )
    da1 = lax.psum_scatter(da1_part, "row", scatter_dimension=0, tiled=True).astype(F32)

    d_qkv = col_scatter_sum(dot_tn(a1, dqkv).astype(BF16))
    d_out = col_scatter_sum(dot_tn(dhb_all, merged).astype(BF16))
    d_att = dp_reduce(jnp.concatenate([d_qkv, d_out], axis=1)).astype(F32)
    small = jnp.concatenate(
        [
            jnp.sum(dnorm_attn, axis=0),
            jnp.sum(dnorm_ffn, axis=0),
            jnp.sum(dgains, axis=2).reshape(-1),
        ]
    )
    small = butterfly_sum(small.reshape(-1, 128), ("col", "row", "dp")).reshape(-1)

    x = x_own.astype(F32)
    r1 = lax.rsqrt(jnp.mean(x * x, axis=-1, keepdims=True) + EPSILON)
    u1 = x * r1
    e1 = da1 * gain_attn
    input_grad = dh + r1 * (e1 - u1 * jnp.mean(e1 * u1, axis=-1, keepdims=True))

    part = norm_attn.shape[0]
    start = lax.axis_index("col") * part
    nqd = nq * HD
    nkd = nkv * HD
    return (
        block_out[None],
        input_grad[None],
        lax.dynamic_slice_in_dim(small[:width], start, part, 0),
        d_att[:, :nqd],
        d_att[:, nqd : nqd + nkd],
        d_att[:, nqd + nkd : nqd + 2 * nkd],
        small[2 * width : 2 * width + HD],
        small[2 * width + HD : 2 * width + 2 * HD],
        d_att[:, nqd + 2 * nkd :].T,
        lax.dynamic_slice_in_dim(small[width : 2 * width], start, part, 0),
        d_ffn[:, :ff],
        d_ffn[:, ff : 2 * ff],
        d_ffn[:, 2 * ff :].T,
    )


def solution(mesh):
    tokens = P(("dp", "col"), "row", None)
    wide = P("col", "row")
    tall = P("row", "col")
    placed = (
        tokens, P(("dp", "col")), P(("dp", "col"), None), P("col"), wide, wide, wide, P(), P(),
        tall, P("col"), wide, wide, tall, tokens,
    )
    return jax.shard_map(
        local,
        mesh=mesh,
        in_specs=placed,
        out_specs=(
            tokens, tokens, P("col"), wide, wide, wide, P(), P(), tall, P("col"), wide, wide, tall,
        ),
        check_vma=False,
    )
```
